32 devices in a mesh: parts: 2 (over x), space: 16 (over z, y, core).
Axes of the slice: x: 2, y: 2, z: 4, core: 2. Of those that a mesh axis runs over, the one named last changes fastest.
Arguments:
- state: float32 [66, 64, 8, 256], P('parts', 'space'), parts along dimension 0, may hold values from 0.25 to 6.5
- adjoint: float32 [64, 64, 8, 256], P('parts', 'space'), parts along dimension 0, may hold values from -6 to 6
- control: float32 [64, 64, 8, 256], P('parts', 'space'), parts along dimension 0, may hold values from -6 to 6
- target: float32 [64, 128], P('parts'), parts along dimension 0, may hold values from 1 to 3
- mask: int32 [64, 16], P('space', 'parts'), parts along dimension 1, may hold values 0 or 1
- regions: int32 [64, 16, 256], P('space', 'parts'), parts along dimension 1, may hold values from 0 to 127, as said below
Outputs:
- state_spectrum: float32 [2, 64, 64, 8, 256], P(None, 'parts', 'space'), parts along dimension 1
- adjoint_spectrum: float32 [2, 64, 64, 8, 256], P(None, 'parts', 'space'), parts along dimension 1
- gradient_residual: float32 [64, 64, 8, 256], P('parts', 'space'), parts along dimension 0
The draws below stay inside these ranges and needn't reach their ends.
There are 2 independent parts, one for each index of `parts`. The reference program is written for one: setup_inputs(seed, part) draws one part's arguments, and reference() takes and returns one part's arrays. A program takes and returns all parts, laid end to end along the dimension named above; each array names one. Nothing has to cross between parts.
Inputs may be any that keep to these rules, and one draw needn't show every extreme that they name: `regions`: every region number from 0 to 127 labels at least one cell.
All inputs are finite; a program needn't handle non-finite values. No bound on the sum of `mask` on one device may be relied on, other than what follows from the above.
Results may differ from the reference program's by a relative error of at most 0.000098.
Values sent between devices are 32-bit elements; how exact they have to be, the bound alone decides.
No kernel may reach another device: no remote copies, remote signals or barrier semaphores. Data moves between devices by JAX's collectives and lax.ppermute only.
A program may use at most 64 MiB of HBM per device.

```python
import jax
import jax.numpy as jnp

ZW = 8
NX = 256
NT = 32
REGIONS = 128
NY = 64


def draw_state(key, part):
    first = jax.random.fold_in(key, 0)
    row_index = jnp.arange(NY, dtype=jnp.float32)
    ramp = (1.0 + 2.0 * row_index / max(NY - 1, 1))[None, :, None, None]
    rough = jax.random.uniform(first, (NT + 1, NY, ZW, NX), jnp.float32, 0.5, 1.5)
    return ramp * rough


def draw_regions(key, part):
    tile_rows = 8
    tile_columns = REGIONS // tile_rows
    key_cuts = jax.random.fold_in(key, 11)
    key_shift = jax.random.fold_in(key, 12)
    key_label = jax.random.fold_in(key, 13)
    shuffled = jax.random.permutation(key_cuts, NY - 1).astype(jnp.int32)
    cut_points = jnp.sort(shuffled[:tile_rows - 1] + 1)
    row_index = jnp.arange(NY, dtype=jnp.int32)
    row_block = jnp.sum((cut_points[None, :] <= row_index[:, None]).astype(jnp.int32), axis=1)
    shifts = jax.random.randint(key_shift, (tile_rows,), 0, NX, dtype=jnp.int32)
    column_index = jnp.arange(NX, dtype=jnp.int32)
    shifted = column_index[None, :] + shifts[:, None]
    column_block = shifted * tile_columns // NX % tile_columns
    labels = jax.random.permutation(key_label, REGIONS).astype(jnp.int32)
    tile_index = row_block[:, None] * tile_columns + column_block[row_block]
    labelled = labels[tile_index]
    return jnp.broadcast_to(labelled[:, None, :], (NY, ZW, NX)).astype(jnp.int32)


def place_ends(entries, key, low, top_value):
    longest = entries.shape.index(max(entries.shape))
    spots = []
    for shift in (0, 1):
        where = [jax.random.randint(jax.random.fold_in(key, axis), (), 0, length) for axis, length in enumerate(entries.shape)]
        where[longest] = (where[longest] + shift) % entries.shape[longest]
        spots.append(tuple(where))
    return entries.at[spots[0]].set(low).at[spots[1]].set(top_value)


def block_scale(stream_key, shape, cuts, least, largest):
    loudness = 1.0
    for position, blocks in cuts:
        draws = jax.random.uniform(jax.random.fold_in(jax.random.fold_in(stream_key, 6), position), (blocks,), jnp.float32, least / len(cuts), largest / len(cuts))
        loudness = loudness * jnp.repeat(jnp.exp(draws), shape[position] // blocks).reshape((-1,) + (1,) * (len(shape) - 1 - position))
    return loudness


def noise(rng, dims, spread, bound, pieces=(), kind=jnp.bfloat16):
    factor_of = block_scale(rng, dims, pieces, -0.22, 0.18) if pieces else 1.0
    array = jax.random.normal(rng, dims, jnp.float32) * spread * factor_of
    return jnp.minimum(jnp.maximum(array, -bound), bound).astype(kind)


def setup_inputs(seed: int = 0, part: int = 0) -> dict:
    key_of = jax.random.split(jax.random.key(seed), 7)
    part_keys = jax.random.split(jax.random.fold_in(key_of[6], part), 7)
    state = draw_state(jax.random.fold_in(jax.random.fold_in(key_of[6], part), 71), part)
    adjoint = noise(part_keys[1], (NT, NY, ZW, NX), 1.0, 6.0, ((1, 16),), jnp.float32)
    control = noise(part_keys[2], (NT, NY, ZW, NX), 1.0, 6.0, ((1, 16),), jnp.float32)
    target = jnp.clip(jax.random.uniform(part_keys[3], (NT, REGIONS), jnp.float32, 1.0, 3.0), 1.0, 3.0)
    mask = place_ends((jax.random.randint(part_keys[4], (NY, ZW), 0, 2) < 1).astype(jnp.int32), jax.random.fold_in(part_keys[4], 1), 0, 1)
    regions = draw_regions(jax.random.fold_in(jax.random.fold_in(key_of[6], part), 71), part)
    return dict(state=state, adjoint=adjoint, control=control, target=target, mask=mask, regions=regions)


time_step = 0.15
penalty = 0.5


def laplace(values):
    across = jnp.roll(values, 1, axis=1) + jnp.roll(values, -1, axis=1)
    padded = jnp.pad(values, ((0, 0), (0, 0), (1, 1), (1, 1)))
    across = across + padded[:, :, 2:, 1:-1] + padded[:, :, :-2, 1:-1]
    across = across + padded[:, :, 1:-1, 2:] + padded[:, :, 1:-1, :-2]
    return across - 6.0 * values


def spectrum(residual):
    transformed = jnp.fft.fft(residual, axis=0)
    return jnp.stack([jnp.real(transformed), jnp.imag(transformed)], 0)


def reference(state, adjoint, control, target, mask, regions):
    support = mask.astype(jnp.float32)[None, :, :, None]
    earlier = state[:-1]
    advanced = state[1:]
    state_res = advanced - earlier - time_step * laplace(earlier) - time_step * support * control
    region_ids = regions.reshape(-1).astype(jnp.int32)
    unit_weight = jnp.ones(region_ids.shape, jnp.float32)
    counts = jax.ops.segment_sum(unit_weight, region_ids, num_segments=REGIONS)
    region_sums = jax.ops.segment_sum(advanced.reshape(NT, -1).T, region_ids, num_segments=REGIONS)
    misfit = region_sums.T / counts - target
    source = misfit[:, region_ids].reshape(advanced.shape)
    following = jnp.concatenate([adjoint[1:], jnp.zeros_like(adjoint[:1])], 0)
    adjoint_res = adjoint - following - time_step * laplace(following) + source
    gradient_residual = penalty * control - support * adjoint
    return spectrum(state_res), spectrum(adjoint_res), gradient_residual
```

```python
import functools
import math

import jax
import jax.numpy as jnp
from jax import lax
from jax.experimental import pallas as pl
from jax.experimental.pallas import tpu as pltpu
from jax.sharding import PartitionSpec as P

time_step = 0.15
penalty = 0.5
lanes = 128


def tiles(values):
    n, rows, planes, columns = values.shape
    split = values.reshape(n, rows, planes, columns // lanes, lanes)
    return jnp.transpose(split, (0, 1, 3, 2, 4))


def untiled(values):
    values = jnp.moveaxis(values, -3, -2)
    return values.reshape(values.shape[:-2] + (-1,))


def real_fft(values):
    n = len(values)
    if n == 1:
        return [(values[0], None)]
    if n == 2:
        return [(values[0] + values[1], None), (values[0] - values[1], None)]
    even, odd = real_fft(values[0::2]), real_fft(values[1::2])
    half = n // 2
    result = [None] * (half + 1)
    for k in range(n // 4 + 1):
        (er, ei), (orr, oi) = even[k], odd[k]
        if k == 0:
            result[0] = (er + orr, None)
            result[half] = (er - orr, None)
        elif 4 * k == n:
            result[k] = (er, -orr)
        else:
            c, s = math.cos(2 * math.pi * k / n), math.sin(2 * math.pi * k / n)
            if oi is None:
                tr, ti = orr * c, orr * (-s)
            elif 8 * k == n:
                tr, ti = (orr + oi) * c, (oi - orr) * c
            else:
                tr, ti = orr * c + oi * s, oi * c - orr * s
            result[k] = (er + tr, ti if ei is None else ei + ti)
            result[half - k] = (er - tr, ti if ei is None else ti - ei)
    return result


def packed(spectrum):
    return [r for r, _ in spectrum] + [i for _, i in spectrum if i is not None]


def store_spectrum(out_ref, reals, where):
    n = len(reals)
    half = n // 2
    for k in range(n):
        m = min(k, n - k)
        out_ref[(0, k) + where] = reals[m]
        if m == 0 or m == half:
            out_ref[(1, k) + where] = jnp.zeros_like(reals[0])
        else:
            imaginary = reals[half + m]
            out_ref[(1, k) + where] = imaginary if k == m else -imaginary


def in_plane(parts):
    depth = parts[0].shape[0]
    plane = lax.broadcasted_iota(jnp.int32, parts[0].shape, 0)
    lane = lax.broadcasted_iota(jnp.int32, parts[0].shape, 1)
    right = [pltpu.roll(v, 1, 1) for v in parts]
    left = [pltpu.roll(v, lanes - 1, 1) for v in parts]
    sums = []
    for i, v in enumerate(parts):
        zero = jnp.zeros_like(v)
        before = right[i - 1] if i else zero
        after = left[i + 1] if i + 1 < len(parts) else zero
        total = jnp.where(lane == 0, before, right[i])
        total = total + jnp.where(lane == lanes - 1, after, left[i])
        total = total + jnp.where(plane == 0, zero, pltpu.roll(v, 1, 0))
        total = total + jnp.where(plane == depth - 1, zero, pltpu.roll(v, depth - 1, 0))
        sums.append(total)
    return sums


def level(ref, j):
    rows, blocks = ref.shape[1:3]
    return [[ref[j, y, b] for b in range(blocks)] for y in range(rows)]


def laplace(now, before, after):
    rows = len(now)
    result = []
    for y in range(rows):
        planes = in_plane(now[y])
        below = now[y - 1] if y else before
        above = now[y + 1] if y + 1 < rows else after
        result.append(
            [p + a + b - 6.0 * v for p, a, b, v in zip(planes, below, above, now[y])]
        )
    return result


def sums_kernel(state_ref, regions_ref, sums_ref):
    levels, rows, blocks, planes, _ = state_ref.shape
    steps = levels - 1
    count_regions = sums_ref.shape[1]
    flat = state_ref.reshape(levels * rows * blocks * planes, lanes)
    cells = rows * blocks * planes
    label = lax.broadcasted_iota(jnp.int32, (count_regions, lanes), 0)
    total = jnp.zeros((3 * steps + 16, count_regions), jnp.float32)
    ones = jnp.ones((16, blocks * lanes), jnp.bfloat16)
    for y in range(rows):
        for z in range(planes):
            left, right = [], []
            for b in range(blocks):
                row = (y * blocks + b) * planes + z
                values = flat[pl.ds(cells + row, steps, stride=cells), :]
                high = values.astype(jnp.bfloat16)
                rest = values - high.astype(jnp.float32)
                middle = rest.astype(jnp.bfloat16)
                low = (rest - middle.astype(jnp.float32)).astype(jnp.bfloat16)
                left.append(jnp.concatenate([high, middle, low], 0))
                ids = regions_ref[y, b, z : z + 1, :]
                right.append(jnp.where(label == ids, 1.0, 0.0).astype(jnp.bfloat16))
            lhs = jnp.concatenate([jnp.concatenate(left, 1), ones], 0)
            total = total + lax.dot_general(
                lhs,
                jnp.concatenate(right, 1),
                (((1,), (1,)), ((), ())),
                preferred_element_type=jnp.float32,
            )
    sums = total[:steps] + total[steps : 2 * steps] + total[2 * steps : 3 * steps]
    sums_ref[...] = jnp.concatenate([sums, total[3 * steps : 3 * steps + 8]], 0)


def state_kernel(
    state_ref, control_ref, support_ref, before_ref, after_ref, out_ref, residual, spectrum, sem
):
    steps, rows, blocks = control_ref.shape[:3]

    def residuals(j, carry):
        now = level(state_ref, j)
        before = [before_ref[j, b] for b in range(blocks)]
        after = [after_ref[j, b] for b in range(blocks)]
        lap = laplace(now, before, after)
        for y in range(rows):
            for b in range(blocks):
                heat = support_ref[y] * control_ref[j, y, b]
                residual[j, y, b] = (
                    state_ref[j + 1, y, b] - now[y][b] - time_step * (lap[y][b] + heat)
                )
        return carry

    lax.fori_loop(0, steps, residuals, 0)

    def copy(y):
        return pltpu.make_async_copy(spectrum.at[:, :, y], out_ref.at[:, :, y], sem.at[y])

    for y in range(rows):
        for b in range(blocks):
            reals = packed(real_fft([residual[j, y, b] for j in range(steps)]))
            store_spectrum(spectrum, reals, (y, b))
        copy(y).start()
    for y in range(rows):
        copy(y).wait()


def adjoint_kernel(adjoint_ref, before_ref, after_ref, out_ref, residual):
    steps, rows, blocks = adjoint_ref.shape[:3]

    def residuals(j, carry):
        now = level(adjoint_ref, j + 1)
        before = [before_ref[j, b] for b in range(blocks)]
        after = [after_ref[j, b] for b in range(blocks)]
        lap = laplace(now, before, after)
        for y in range(rows):
            for b in range(blocks):
                residual[j, y, b] = adjoint_ref[j, y, b] - now[y][b] - time_step * lap[y][b]
        return carry

    lax.fori_loop(0, steps - 1, residuals, 0)
    for y in range(rows):
        for b in range(blocks):
            values = [residual[j, y, b] for j in range(steps - 1)] + [adjoint_ref[steps - 1, y, b]]
            for k, real in enumerate(packed(real_fft(values))):
                out_ref[k, y, b] = real


def source_kernel(partial_ref, sums_ref, target_ref, regions_ref, out_ref, table, spectrum, sem):
    steps, rows, blocks, planes, _ = partial_ref.shape
    count_regions = target_ref.shape[1]
    counts = sums_ref[steps : steps + 1, :]
    misfit = sums_ref[:steps, :] / counts - target_ref[...]
    for k, real in enumerate(packed(real_fft([misfit[j : j + 1] for j in range(steps)]))):
        table[k : k + 1, :] = real

    def copy(y):
        return pltpu.make_async_copy(spectrum.at[:, :, y], out_ref.at[:, :, y], sem.at[y])

    for y in range(rows):
        for b in range(blocks):
            ids = regions_ref[y, b]
            reals = []
            for k in range(steps):
                total = partial_ref[k, y, b]
                for first in range(0, count_regions, lanes):
                    row = jnp.broadcast_to(table[k : k + 1, first : first + lanes], (planes, lanes))
                    local = ids - first if count_regions > lanes else ids
                    inside = jnp.clip(local, 0, lanes - 1) if count_regions > lanes else local
                    found = jnp.take_along_axis(row, inside, axis=1)
                    if count_regions > lanes:
                        found = jnp.where(inside == local, found, 0.0)
                    total = total + found
                reals.append(total)
            store_spectrum(spectrum, reals, (y, b))
        copy(y).start()
    for y in range(rows):
        copy(y).wait()


vmem = pl.BlockSpec(memory_space=pltpu.VMEM)
anywhere = pl.BlockSpec(memory_space=pl.ANY)


def call(kernel, out_shape, out_spec, scratch, count, name, cost):
    return pl.pallas_call(
        kernel,
        out_shape=jax.ShapeDtypeStruct(out_shape, jnp.float32),
        in_specs=[vmem] * count,
        out_specs=out_spec,
        scratch_shapes=scratch,
        name=name,
        compiler_params=pltpu.CompilerParams(vmem_limit_bytes=24 * 1024 * 1024),
        cost_estimate=pl.CostEstimate(flops=cost, bytes_accessed=cost, transcendentals=0),
    )


def on_device(state, adjoint, control, target, mask, regions):
    count_steps = control.shape[0]
    count_regions = target.shape[1]
    support = mask.astype(jnp.float32)
    gradient_residual = penalty * control - support[None, :, :, None] * adjoint
    count = lax.axis_size("space")
    up = [(i, (i + 1) % count) for i in range(count)]
    down = [(j, i) for i, j in up]
    state, adjoint, control = tiles(state), tiles(adjoint), tiles(control)
    regions = tiles(regions[None])[0]
    rows, blocks, planes = control.shape[1:4]
    support = jnp.broadcast_to(support[:, :, None], (rows, planes, lanes))

    state_before = lax.ppermute(state[:-1, -1], "space", up)
    state_after = lax.ppermute(state[:-1, 0], "space", down)
    adjoint_before = lax.ppermute(adjoint[1:, -1], "space", up)
    adjoint_after = lax.ppermute(adjoint[1:, 0], "space", down)

    sums = call(
        sums_kernel, (count_steps + 8, count_regions), vmem, [], 2, "region_sums", 4 << 20
    )(state, regions)
    width = 1
    while width < count:
        sums = sums + lax.ppermute(sums, "space", [(i, i ^ width) for i in range(count)])
        width *= 2

    spectrum_shape = (2,) + control.shape
    big = [pltpu.VMEM(control.shape, jnp.float32), pltpu.VMEM(spectrum_shape, jnp.float32)]
    sems = [pltpu.SemaphoreType.DMA((rows,))]
    state_spectrum = call(
        state_kernel, spectrum_shape, anywhere, big + sems, 5, "state_spectrum", 4 << 20
    )(state, control, support, state_before, state_after)
    partial = call(
        adjoint_kernel, adjoint.shape, vmem, big[:1], 3, "adjoint_partial", 4 << 20
    )(adjoint, adjoint_before, adjoint_after)
    adjoint_spectrum = call(
        source_kernel,
        spectrum_shape,
        anywhere,
        [pltpu.VMEM((count_steps, count_regions), jnp.float32)] + big[1:] + sems,
        4,
        "adjoint_spectrum",
        4 << 20,
    )(partial, sums, target, regions)
    return untiled(state_spectrum), untiled(adjoint_spectrum), gradient_residual


def solution(mesh):
    return jax.shard_map(
        on_device,
        mesh=mesh,
        in_specs=(
            P("parts", "space", None, None),
            P("parts", "space", None, None),
            P("parts", "space", None, None),
            P("parts", None),
            P("space", "parts"),
            P("space", "parts", None),
        ),
        out_specs=(
            P(None, "parts", "space", None, None),
            P(None, "parts", "space", None, None),
            P("parts", "space", None, None),
        ),
        check_vma=False,
    )
```
